32 devices in a mesh: layer: 4 (over y, core), front: 8 (over z, x).
Axes of the slice: x: 2, y: 2, z: 4, core: 2. Of those that a mesh axis runs over, the one named last changes fastest.
Arguments:
- child_rhs: bfloat16 [4, 2, 48, 8192], P('layer', None, None, 'front'), may hold values from -6 to 6
- parent_rhs: bfloat16 [4, 2, 48, 4096], P('layer', None, None, 'front'), may hold values from -6 to 6
- root_rhs: bfloat16 [4, 2, 48, 4096], P('layer', None, None, 'front'), may hold values from -6 to 6
- child_inverse: bfloat16 [4, 2048, 8192], P('layer', None, 'front'), as said below
- child_update: bfloat16 [4, 8192, 2048], P('layer', 'front'), may hold values from -0.125 to 0.125
- parent_inverse: bfloat16 [4, 2048, 4096], P('layer', None, 'front'), as said below
- parent_update: bfloat16 [4, 4096, 3072], P('layer', 'front'), may hold values from -0.125 to 0.125
- root_inverse: bfloat16 [4, 4096, 4096], P('layer', None, 'front'), as said below
- coupling: float32 [4, 4096], P('layer', 'front'), may hold values from 0.25 to 1
- child_map: int32 [4, 2048], replicated, may hold values from 0 to 6143, as said below
- parent_map: int32 [2, 3072], replicated, may hold values from 0 to 4095, as said below
Outputs:
- solution: bfloat16 [4, 2, 48, 4096], P('layer', None, None, 'front')
The draws below stay inside these ranges and needn't reach their ends.
Inputs may be any that keep to these rules, and one draw needn't show every extreme that they name: `child_map`: each row holds 2048 distinct entries; values below 2048 name rows of the parent front's separator, the others name row value - 2048 of the top separator. `parent_map`: each row holds 3072 distinct rows of the top separator. `child_inverse`: each group's matrix, read as rows k and columns f * 2048 + j, is zero where k > j. `parent_inverse`: each group's matrix, read as rows k and columns f * 2048 + j, is zero where k > j. `root_inverse`: each group's matrix is zero below its diagonal.
All inputs are finite; a program needn't handle non-finite values.
Results may differ from the reference program's by a relative error of at most 0.02.
Values may be sent and summed in bfloat16 or wider, within the bound.
No kernel may reach another device: no remote copies, remote signals or barrier semaphores. Data moves between devices by JAX's collectives and lax.ppermute only.
A program may use at most 64 MiB of HBM per device.

```python
import math
import jax
import jax.numpy as jnp
from jax import lax

S0 = 4096
S1 = 2048
U1 = 3072
S2 = 2048
U2 = 2048
RHS = 48
GROUPS = 4
N_FRONT = 8


def lower_factor(key, front_count, front_size):
    noise_key, diag_key = jax.random.split(jax.random.fold_in(key, 7))
    shape = (GROUPS, front_size, front_count, front_size)
    noise = jax.random.normal(noise_key, shape, jnp.float32)
    k_index = lax.broadcasted_iota(jnp.int32, (1, front_size, 1, front_size), 1)
    j_index = lax.broadcasted_iota(jnp.int32, (1, front_size, 1, front_size), 3)
    below = (k_index < j_index).astype(jnp.float32)
    on_diag = (k_index == j_index).astype(jnp.float32)
    diag_values = jax.random.uniform(diag_key, (GROUPS, 1, front_count, front_size), jnp.float32, 0.7, 1.3)
    values = noise * below * (0.8 / front_size ** 0.5) + on_diag * diag_values
    return values.reshape(GROUPS, front_size, front_count * front_size).astype(jnp.bfloat16)


def draw_child_inverse(key, part):
    return lower_factor(jax.random.fold_in(key, 21), 4, S2)


def draw_parent_inverse(key, part):
    return lower_factor(jax.random.fold_in(key, 22), 2, S1)


def draw_root_inverse(key, part):
    return lower_factor(jax.random.fold_in(key, 23), 1, S0)


def draw_child_map(key, part):
    keys = jax.random.split(jax.random.fold_in(key, 31), 4)
    return jax.vmap(lambda each_key: jax.random.permutation(each_key, S1 + S0)[:U2])(keys).astype(jnp.int32)


def draw_parent_map(key, part):
    keys = jax.random.split(jax.random.fold_in(key, 32), 2)
    return jax.vmap(lambda each_key: jax.random.permutation(each_key, S0)[:U1])(keys).astype(jnp.int32)


def shard_levels(rng, extent, cuts, low, high):
    gain = 1.0
    for axis_at, blocks in cuts:
        heights = jax.random.uniform(jax.random.fold_in(jax.random.fold_in(rng, 6), axis_at), (blocks,), jnp.float32, low / len(cuts), high / len(cuts))
        gain = gain * jnp.repeat(jnp.exp(heights), extent[axis_at] // blocks).reshape((-1,) + (1,) * (len(extent) - 1 - axis_at))
    return gain


def scatter_about(rng, extent, deviation, bound, pieces=(), held_as=jnp.bfloat16):
    entries = jax.random.normal(rng, extent, jnp.float32) * deviation
    if len(pieces) > 0:
        entries = shard_levels(rng, extent, pieces, -0.22, 0.18) * entries
    return jnp.clip(entries, min=-bound, max=bound).astype(held_as)


def setup_inputs(seed: int = 0) -> dict:
    seeds = jax.random.split(jax.random.key(seed), 12)
    child_rhs = scatter_about(seeds[0], (GROUPS, 2, RHS, 4 * S2), 1.0, 6.0, ((0, 4), (3, 8)))
    parent_rhs = scatter_about(seeds[1], (GROUPS, 2, RHS, 2 * S1), 1.0, 6.0, ((0, 4), (3, 8)))
    root_rhs = scatter_about(seeds[2], (GROUPS, 2, RHS, S0), 1.0, 6.0, ((0, 4), (3, 8)))
    child_inverse = draw_child_inverse(jax.random.fold_in(seeds[11], 71), 0)
    child_update = scatter_about(seeds[4], (GROUPS, 4 * S2, U2), S2 ** -0.5, 0.125, ((0, 4), (1, 8)))
    parent_inverse = draw_parent_inverse(jax.random.fold_in(seeds[11], 71), 0)
    parent_update = scatter_about(seeds[6], (GROUPS, 2 * S1, U1), S1 ** -0.5, 0.125, ((0, 4), (1, 8)))
    root_inverse = draw_root_inverse(jax.random.fold_in(seeds[11], 71), 0)
    coupling = jnp.clip(jnp.exp(math.log(1.0) - 1.3862944 * jax.random.uniform(seeds[8], (GROUPS, S0), jnp.float32) ** shard_levels(seeds[8], (GROUPS, S0), ((0, 4), (1, 8)), -0.2, 0.2)), 0.25, 1.0)
    child_map = draw_child_map(jax.random.fold_in(seeds[11], 71), 0)
    parent_map = draw_parent_map(jax.random.fold_in(seeds[11], 71), 0)
    return dict(child_rhs=child_rhs, parent_rhs=parent_rhs, root_rhs=root_rhs, child_inverse=child_inverse, child_update=child_update, parent_inverse=parent_inverse, parent_update=parent_update, root_inverse=root_inverse, coupling=coupling, child_map=child_map, parent_map=parent_map)


def front_solve(rhs_cols, inverse, front_count):
    row_count = rhs_cols.shape[0]
    front_size = inverse.shape[0]
    blocks = rhs_cols.reshape(row_count, front_count, front_size).astype(jnp.float32)
    factor = inverse.reshape(front_size, front_count, front_size).astype(jnp.float32)
    solved = jnp.einsum("rfk,kfj->rfj", blocks, factor)
    return solved.reshape(row_count, front_count * front_size).astype(jnp.bfloat16)


def share_terms(solved, update):
    row_count = solved.shape[0]
    share_width = solved.shape[1] // N_FRONT
    left_part = solved.reshape(row_count, N_FRONT, share_width).astype(jnp.float32)
    right_part = update.reshape(N_FRONT, share_width, update.shape[1]).astype(jnp.float32)
    return jnp.einsum("rdw,dwu->dru", left_part, right_part)


def place_terms(terms, targets, target_width):
    def place_one(term_block, target_row):
        empty = jnp.zeros((term_block.shape[0], target_width), jnp.float32)
        return empty.at[:, target_row].add(term_block, mode="drop")
    return jax.vmap(place_one)(terms, targets)


def rounded_sum(terms):
    narrow = lax.optimization_barrier(terms.astype(jnp.bfloat16))
    return jnp.sum(narrow.astype(jnp.float32), axis=0)


def group_solve(group_args, child_map, parent_map):
    child_rhs, parent_rhs, root_rhs, incoming, child_inverse, child_update, parent_inverse, parent_update, root_inverse, coupling = group_args
    row_count = child_rhs.shape[0]
    device_ids = jnp.arange(N_FRONT, dtype=jnp.int32)
    child_front = device_ids // (N_FRONT // 4)
    child_targets = child_map[child_front].astype(jnp.int32)
    to_parent = jnp.where(child_targets < S1, (child_front[:, None] // 2) * S1 + child_targets, 2 * S1).astype(jnp.int32)
    to_root = jnp.where(child_targets >= S1, child_targets - S1, S0).astype(jnp.int32)
    child_solved = front_solve(child_rhs, child_inverse, 4)
    child_terms = share_terms(child_solved, child_update)
    parent_sum = rounded_sum(place_terms(child_terms, to_parent, 2 * S1))
    parent_now = (parent_rhs.astype(jnp.float32) - parent_sum).astype(jnp.bfloat16)
    parent_solved = front_solve(parent_now, parent_inverse, 2)
    parent_terms = share_terms(parent_solved, parent_update)
    parent_targets = parent_map[device_ids // (N_FRONT // 2)].astype(jnp.int32)
    root_terms = place_terms(child_terms, to_root, S0) + place_terms(parent_terms, parent_targets, S0)
    share_width = S0 // N_FRONT
    own_cols = (incoming.astype(jnp.float32) - root_rhs.astype(jnp.float32)).reshape(1, row_count, N_FRONT, share_width)
    picker = jnp.eye(N_FRONT, dtype=jnp.float32)
    placed = (picker[:, None, :, None] * own_cols).reshape(N_FRONT, row_count, S0)
    root_now = (-rounded_sum(root_terms + placed)).astype(jnp.bfloat16)
    root_solved = jnp.dot(root_now, root_inverse, preferred_element_type=jnp.float32)
    return root_solved.astype(jnp.bfloat16), (coupling[None, :] * root_solved).astype(jnp.bfloat16)


def reference(child_rhs, parent_rhs, root_rhs, child_inverse, child_update, parent_inverse, parent_update, root_inverse, coupling, child_map, parent_map):
    def run_block(block_id, incoming):
        def per_group(group_args):
            return group_solve(group_args, child_map, parent_map)
        return lax.map(per_group, (child_rhs[:, block_id], parent_rhs[:, block_id], root_rhs[:, block_id], incoming, child_inverse, child_update, parent_inverse, parent_update, root_inverse, coupling))

    silent = jnp.zeros(root_rhs[:, 0].shape, jnp.bfloat16)
    first_sol, outgoing = run_block(0, silent)
    incoming = jnp.concatenate([silent[:1], outgoing[:-1]], axis=0)
    second_sol, leftover = run_block(1, incoming)
    return jnp.stack([first_sol, second_sol], axis=1)
```

```python
import functools

import jax
import jax.numpy as jnp
from jax import lax
from jax.experimental import pallas as pl
from jax.experimental.pallas import tpu as pltpu
from jax.sharding import PartitionSpec as P


LOW = 256
BF = jnp.bfloat16
F32 = jnp.float32
WHOLE = pl.BlockSpec(memory_space=pltpu.VMEM)


def call(kernel, name, outs, scratch, limit, cost, *args):
    return pl.pallas_call(
        kernel,
        name=name,
        out_shape=[jax.ShapeDtypeStruct(shape, dtype) for shape, dtype in outs],
        in_specs=[WHOLE] * len(args),
        out_specs=[WHOLE] * len(outs),
        scratch_shapes=scratch,
        compiler_params=pltpu.CompilerParams(vmem_limit_bytes=limit),
        cost_estimate=pl.CostEstimate(flops=cost[0], bytes_accessed=cost[1], transcendentals=0),
    )(*args)


def one_hot_rows(columns, low_ref):
    width = columns.shape[1]
    lane = lax.broadcasted_iota(jnp.int32, (LOW, width), 0)
    low_ref[...] = jnp.where(lane == (columns & (LOW - 1)), 1.0, 0.0).astype(BF)


def place_columns(values, columns, first, blocks, low_ref, stack_ref, put):
    rows = values.shape[0]
    high = columns // LOW
    together = stack_ref.shape[0] // rows
    for start in range(0, blocks, together):
        count = min(together, blocks - start)
        for j in range(count):
            here = jnp.where(high == first + start + j, 1.0, 0.0).astype(BF)
            stack_ref[j * rows : (j + 1) * rows, :] = values * here
        placed = lax.dot_general(
            stack_ref[: count * rows, :],
            low_ref[...],
            (((1,), (1,)), ((), ())),
            preferred_element_type=F32,
        )
        for j in range(count):
            put(start + j, placed[j * rows : (j + 1) * rows])


def shared_dot(pieces, weights, position, width, offset=0):
    total = None
    for k, piece in enumerate(pieces):
        first = pl.multiple_of(offset + (position ^ k) * width, width)
        part = jnp.dot(piece, weights[pl.ds(first, width), :], preferred_element_type=F32)
        total = part if total is None else total + part
    return total


def child_kernel(pieces, members, group, where, *refs):
    piece_refs = refs[:pieces]
    inverse, update, maps = refs[pieces : pieces + 3]
    sends = refs[pieces + 3 : pieces + 3 + group]
    terms, low, stack, summed = refs[pieces + 3 + group :]
    device = where()
    front, place, member = device // members, device % members, device % group
    solved = shared_dot([r[...] for r in piece_refs], inverse, place, piece_refs[0].shape[1])
    solved = solved.astype(BF)
    for start in range(0, update.shape[1], 512):
        terms[:, start : start + 512] = jnp.dot(
            solved, update[:, start : start + 512], preferred_element_type=F32
        ).astype(BF)
    columns = maps[pl.ds(front, 1), :]
    one_hot_rows(columns, low)

    def put(block, value):
        summed[:, block * LOW : (block + 1) * LOW] = value.astype(BF)

    place_columns(terms[...], columns, 0, summed.shape[1] // LOW, low, stack, put)
    width = sends[0].shape[1]
    for k, send in enumerate(sends):
        send[...] = summed[:, pl.ds(pl.multiple_of((member ^ k) * width, width), width)]


def child_root_kernel(members, parent_blocks, where, terms, maps, placed_ref, low, stack):
    columns = maps[pl.ds(where() // members, 1), :]
    one_hot_rows(columns, low)

    def put(block, value):
        placed_ref[:, block * LOW : (block + 1) * LOW] = value.astype(BF)

    place_columns(
        terms[...], columns, parent_blocks, placed_ref.shape[1] // LOW, low, stack, put
    )


def parent_kernel(group, where, *refs):
    piece_refs = refs[:group]
    inverse, update, maps, child_root = refs[group : group + 4]
    sends0 = refs[group + 4 : 2 * group + 4]
    sends1 = refs[2 * group + 4 : 3 * group + 4]
    terms, low, stack, total = refs[3 * group + 4 :]
    device = where()
    front, member = device // group, device % group
    solved = shared_dot([r[...] for r in piece_refs], inverse, member, piece_refs[0].shape[1])
    solved = solved.astype(BF)
    for start in range(0, update.shape[1], 512):
        terms[:, start : start + 512] = jnp.dot(
            solved, update[:, start : start + 512], preferred_element_type=F32
        ).astype(BF)
    columns = maps[pl.ds(front, 1), :]
    one_hot_rows(columns, low)

    def put(block, value):
        here = slice(block * LOW, (block + 1) * LOW)
        total[:, here] = (value + child_root[:, here].astype(F32)).astype(BF)

    place_columns(terms[...], columns, 0, total.shape[1] // LOW, low, stack, put)
    rows, width = sends0[0].shape[0], sends0[0].shape[1] // 2
    half = total.shape[1] // 2
    for k in range(group):
        first = pl.multiple_of((member ^ k) * width, width)
        second = pl.multiple_of(half + (member ^ k) * width, width)
        for base, sends in ((0, sends0), (rows, sends1)):
            sends[k][:, :width] = total[base : base + rows, pl.ds(first, width)]
            sends[k][:, width:] = total[base : base + rows, pl.ds(second, width)]


def root_dot(group, where, piece_refs, inverse):
    member = where() % group
    width = piece_refs[0].shape[1] // 2
    lower = shared_dot([r[:, :width] for r in piece_refs], inverse, member, width)
    upper = shared_dot(
        [r[:, width:] for r in piece_refs], inverse, member, width, inverse.shape[0] // 2
    )
    return lower + upper


def first_root_kernel(group, where, *refs):
    piece_refs, (inverse, coupling, solved_ref, hand_ref) = refs[:group], refs[group:]
    solved = root_dot(group, where, piece_refs, inverse)
    solved_ref[...] = solved.astype(BF)
    hand_ref[...] = (coupling[...] * solved).astype(BF)


def second_root_kernel(group, where, *refs):
    piece_refs, (inverse, first_ref, out_ref) = refs[:group], refs[group:]
    solved = root_dot(group, where, piece_refs, inverse)
    rows = first_ref.shape[0]
    out_ref[:rows, :] = first_ref[...]
    out_ref[rows:, :] = solved.astype(BF)


def body(
    child_rhs,
    parent_rhs,
    root_rhs,
    child_inverse,
    child_update,
    parent_inverse,
    parent_update,
    root_inverse,
    coupling,
    child_map,
    parent_map,
):
    devices = lax.axis_size("front")
    layers = lax.axis_size("layer")
    members = devices // child_map.shape[0]
    group = devices // parent_map.shape[0]
    rows = child_rhs.shape[2]
    both = 2 * rows
    root_size = root_inverse.shape[1]
    parent_size = parent_inverse.shape[1]
    front_index = lax.axis_index("front")
    where = functools.partial(lax.axis_index, "front")
    upper = front_index >= group

    def trade(value, k):
        return lax.ppermute(value, "front", [(d, d ^ k) for d in range(devices)])

    def climb(value, k, size):
        pairs = [(d, d ^ k) for d in range(devices) if (d ^ k) % size > d % size]
        return lax.ppermute(value, "front", pairs)

    rhs = child_rhs[0].reshape(both, child_rhs.shape[3])
    pieces = [rhs] + [climb(rhs, k, members) for k in range(1, members)]
    child_width = child_update.shape[2]
    share = parent_size // group
    *sends, terms = call(
        functools.partial(child_kernel, members, members, group, where),
        "child",
        [((both, share), BF)] * group + [((both, child_width), BF)],
        [
            pltpu.VMEM((LOW, child_width), BF),
            pltpu.VMEM((4 * both, child_width), BF),
            pltpu.VMEM((both, parent_size), BF),
        ],
        12 << 20,
        (both * 2 * child_inverse.size * 2, child_inverse.size * 4),
        *pieces,
        child_inverse[0],
        child_update[0],
        child_map,
    )
    (child_root,) = call(
        functools.partial(child_root_kernel, members, parent_size // LOW, where),
        "child_root",
        [((both, root_size), BF)],
        [pltpu.VMEM((LOW, child_width), BF), pltpu.VMEM((4 * both, child_width), BF)],
        10 << 20,
        (both * 2 * root_size * child_width, root_size * both * 4),
        terms,
        child_map,
    )
    summed = sends[0].astype(F32)
    for k in range(1, group):
        summed = summed + trade(sends[k], k).astype(F32)
    parent_now = (
        parent_rhs[0].reshape(both, parent_rhs.shape[3]).astype(F32) - summed
    ).astype(BF)
    pieces = [parent_now] + [climb(parent_now, k, group) for k in range(1, group)]
    parent_width = parent_update.shape[2]
    root_share = root_size // devices
    sends = call(
        functools.partial(parent_kernel, group, where),
        "parent",
        [((rows, 2 * root_share), BF)] * (2 * group),
        [
            pltpu.VMEM((both, parent_width), BF),
            pltpu.VMEM((LOW, parent_width), BF),
            pltpu.VMEM((4 * both, parent_width), BF),
            pltpu.VMEM((both, root_size), BF),
        ],
        14 << 20,
        (both * 2 * root_size * parent_width, parent_update.size * 4),
        *pieces,
        parent_inverse[0],
        parent_update[0],
        parent_map,
        child_root,
    )

    def own_rhs(block):
        value = root_rhs[0, block].astype(F32)
        blank = jnp.zeros_like(value)
        return jnp.concatenate(
            [jnp.where(upper, blank, value), jnp.where(upper, value, blank)], 1
        )

    def group_sum(parts, block):
        total = parts[0].astype(F32)
        for k in range(1, group):
            total = total + trade(parts[k], k).astype(F32)
        return total - own_rhs(block)

    def halves(lower, higher):
        return jnp.concatenate([lower, jnp.where(upper, higher, jnp.zeros_like(higher))], 1)

    def gathered(now):
        return [now] + [trade(now, k) for k in range(1, group)]

    def crossed(part):
        return part + trade(part.astype(BF), group).astype(F32)

    root_cost = (rows * 2 * root_inverse.size, root_inverse.size * 2)
    total = crossed(group_sum(sends[:group], 0))
    now = -halves(total[:, :root_share], total[:, root_share:])
    first_sol, outgoing = call(
        functools.partial(first_root_kernel, group, where),
        "root_first",
        [((rows, root_share), BF), ((rows, root_share), BF)],
        [],
        4 << 20,
        root_cost,
        *gathered(now.astype(BF)),
        root_inverse[0],
        coupling,
    )
    same = [
        (layer * devices + d, (layer + 1) * devices + d)
        for layer in range(layers - 1)
        for d in range(devices)
    ]
    over = [
        (layer * devices + d, (layer + 1) * devices + group + d)
        for layer in range(layers - 1)
        for d in range(group)
    ]
    incoming = lax.ppermute(outgoing, ("layer", "front"), same).astype(F32)
    beside = lax.ppermute(outgoing, ("layer", "front"), over).astype(F32)
    total = crossed(group_sum(sends[group:], 1))
    lower = total[:, :root_share] + jnp.where(upper, beside, incoming)
    now = -halves(lower, total[:, root_share:] + incoming)
    (out,) = call(
        functools.partial(second_root_kernel, group, where),
        "root_second",
        [((both, root_share), BF)],
        [],
        4 << 20,
        root_cost,
        *gathered(now.astype(BF)),
        root_inverse[0],
        first_sol,
    )
    return out.reshape(1, 2, rows, root_share)


def solution(mesh):
    placed = (
        P("layer", None, None, "front"),
        P("layer", None, None, "front"),
        P("layer", None, None, "front"),
        P("layer", None, "front"),
        P("layer", "front", None),
        P("layer", None, "front"),
        P("layer", "front", None),
        P("layer", None, "front"),
        P("layer", "front"),
        P(),
        P(),
    )
    return jax.shard_map(
        body, mesh=mesh, in_specs=placed, out_specs=P("layer", None, None, "front"), check_vma=False
    )
```

```python
import functools

import jax
import jax.numpy as jnp
from jax import lax
from jax.experimental import pallas as pl
from jax.experimental.pallas import tpu as pltpu
from jax.sharding import PartitionSpec as P


LOW = 256
BF = jnp.bfloat16
F32 = jnp.float32
WHOLE = pl.BlockSpec(memory_space=pltpu.VMEM)


def call(kernel, name, outs, scratch, limit, cost, *args):
    return pl.pallas_call(
        kernel,
        name=name,
        out_shape=[jax.ShapeDtypeStruct(shape, dtype) for shape, dtype in outs],
        in_specs=[WHOLE] * len(args),
        out_specs=[WHOLE] * len(outs),
        scratch_shapes=scratch,
        compiler_params=pltpu.CompilerParams(vmem_limit_bytes=limit),
        cost_estimate=pl.CostEstimate(flops=cost[0], bytes_accessed=cost[1], transcendentals=0),
    )(*args)


def one_hot_rows(columns, low_ref):
    width = columns.shape[1]
    lane = lax.broadcasted_iota(jnp.int32, (LOW, width), 0)
    low_ref[...] = jnp.where(lane == (columns & (LOW - 1)), 1.0, 0.0).astype(BF)


def place_columns(values, columns, first, blocks, low_ref, stack_ref, put):
    rows = values.shape[0]
    high = columns // LOW
    together = stack_ref.shape[0] // rows
    for start in range(0, blocks, together):
        count = min(together, blocks - start)
        for j in range(count):
            here = jnp.where(high == first + start + j, 1.0, 0.0).astype(BF)
            stack_ref[j * rows : (j + 1) * rows, :] = values * here
        placed = lax.dot_general(
            stack_ref[: count * rows, :],
            low_ref[...],
            (((1,), (1,)), ((), ())),
            preferred_element_type=F32,
        )
        for j in range(count):
            put(start + j, placed[j * rows : (j + 1) * rows])


def shared_dot(pieces, weights, position, width, offset=0):
    total = None
    for k, piece in enumerate(pieces):
        first = pl.multiple_of(offset + (position ^ k) * width, width)
        part = jnp.dot(piece, weights[pl.ds(first, width), :], preferred_element_type=F32)
        total = part if total is None else total + part
    return total


def load_kernel(members, group, where, layer, *refs):
    (inverse, update, rhs, child_maps, parent_maps, root_rhs) = refs[:6]
    (inverse_v, update_v, partial, child_low, parent_low, columns, parent_columns) = refs[6:13]
    (placed_rhs, keep, lower_in, upper_in) = refs[13:17]
    rhs_v, child_maps_v, parent_maps_v, root_rhs_v, sems = refs[17:]
    pairs = (
        (child_maps, child_maps_v),
        (parent_maps, parent_maps_v),
        (root_rhs, root_rhs_v),
        (rhs, rhs_v),
        (inverse, inverse_v),
        (update, update_v),
    )
    copies = [pltpu.make_async_copy(a, b, sems.at[i]) for i, (a, b) in enumerate(pairs)]
    for copy in copies:
        copy.start()
    device = where()
    upper = device >= group
    copies[0].wait()
    columns[...] = child_maps_v[pl.ds(device // members, 1), :]
    one_hot_rows(columns[...], child_low)
    copies[1].wait()
    parent_columns[...] = parent_maps_v[pl.ds(device // group, 1), :]
    one_hot_rows(parent_columns[...], parent_low)
    copies[2].wait()
    width = root_rhs.shape[1]
    value = root_rhs_v[...].astype(F32)
    placed_rhs[:, :width] = jnp.where(upper, 0.0, value)
    placed_rhs[:, width:] = jnp.where(upper, value, 0.0)
    keep[:, :width] = jnp.ones((1, width), F32)
    above = jnp.where(upper, 1.0, 0.0)
    inside = jnp.where(layer() > 0, 1.0, 0.0)
    keep[:, width:] = jnp.full((1, width), above, F32)
    lower_in[...] = jnp.full((1, width), inside * (1.0 - above), F32)
    upper_in[...] = jnp.full((1, width), inside * above, F32)
    copies[3].wait()
    copies[4].wait()
    depth = rhs.shape[1]
    own = pl.multiple_of((device % members) * depth, depth)
    partial[...] = jnp.dot(
        rhs_v[...], inverse_v[pl.ds(own, depth), :], preferred_element_type=F32
    )
    copies[5].wait()


def child_kernel(pieces, members, group, where, *refs):
    piece_refs = refs[:pieces]
    partial, inverse, update, columns, low = refs[pieces : pieces + 5]
    sends = refs[pieces + 5 : pieces + 5 + group]
    terms, stack, summed = refs[pieces + 5 + group :]
    device = where()
    place, member = device % members, device % group
    solved = partial[...]
    for k, piece in enumerate(piece_refs, 1):
        depth = piece.shape[1]
        first = pl.multiple_of((place ^ k) * depth, depth)
        solved = solved + jnp.dot(
            piece[...], inverse[pl.ds(first, depth), :], preferred_element_type=F32
        )
    solved = solved.astype(BF)
    for start in range(0, update.shape[1], 512):
        terms[:, start : start + 512] = jnp.dot(
            solved, update[:, start : start + 512], preferred_element_type=F32
        ).astype(BF)

    def put(block, value):
        summed[:, block * LOW : (block + 1) * LOW] = value.astype(BF)

    place_columns(terms[...], columns[...], 0, summed.shape[1] // LOW, low, stack, put)
    width = sends[0].shape[1]
    for k, send in enumerate(sends):
        send[...] = summed[:, pl.ds(pl.multiple_of((member ^ k) * width, width), width)]


def child_root_kernel(parent_blocks, terms, columns, low, placed_ref, stack):
    def put(block, value):
        placed_ref[:, block * LOW : (block + 1) * LOW] = value.astype(BF)

    place_columns(
        terms[...], columns[...], parent_blocks, placed_ref.shape[1] // LOW, low, stack, put
    )


def parent_kernel(group, where, *refs):
    piece_refs = refs[:group]
    inverse, update, columns, low, child_root = refs[group : group + 5]
    sends0 = refs[group + 5 : 2 * group + 5]
    sends1 = refs[2 * group + 5 : 3 * group + 5]
    terms, stack, total = refs[3 * group + 5 :]
    member = where() % group
    solved = shared_dot([r[...] for r in piece_refs], inverse, member, piece_refs[0].shape[1])
    solved = solved.astype(BF)
    for start in range(0, update.shape[1], 512):
        terms[:, start : start + 512] = jnp.dot(
            solved, update[:, start : start + 512], preferred_element_type=F32
        ).astype(BF)

    def put(block, value):
        here = slice(block * LOW, (block + 1) * LOW)
        total[:, here] = (value + child_root[:, here].astype(F32)).astype(BF)

    place_columns(terms[...], columns[...], 0, total.shape[1] // LOW, low, stack, put)
    rows, width = sends0[0].shape[0], sends0[0].shape[1] // 2
    half = total.shape[1] // 2
    for k in range(group):
        first = pl.multiple_of((member ^ k) * width, width)
        second = pl.multiple_of(half + (member ^ k) * width, width)
        for base, sends in ((0, sends0), (rows, sends1)):
            sends[k][:, :width] = total[base : base + rows, pl.ds(first, width)]
            sends[k][:, width:] = total[base : base + rows, pl.ds(second, width)]


def root_dot(group, where, piece_refs, inverse):
    member = where() % group
    width = piece_refs[0].shape[1] // 2
    lower = shared_dot([r[:, :width] for r in piece_refs], inverse, member, width)
    upper = shared_dot(
        [r[:, width:] for r in piece_refs], inverse, member, width, inverse.shape[0] // 2
    )
    return lower + upper


def first_root_kernel(group, where, *refs):
    piece_refs, (inverse, coupling, solved_ref, hand_ref) = refs[:group], refs[group:]
    solved = root_dot(group, where, piece_refs, inverse)
    solved_ref[...] = solved.astype(BF)
    hand_ref[...] = (coupling[...] * solved).astype(BF)


def second_root_kernel(group, where, *refs):
    piece_refs, (inverse, first_ref, out_ref) = refs[:group], refs[group:]
    solved = root_dot(group, where, piece_refs, inverse)
    rows = first_ref.shape[0]
    out_ref[:rows, :] = first_ref[...]
    out_ref[rows:, :] = solved.astype(BF)


def body(
    child_rhs,
    parent_rhs,
    root_rhs,
    child_inverse,
    child_update,
    parent_inverse,
    parent_update,
    root_inverse,
    coupling,
    child_map,
    parent_map,
):
    devices = lax.axis_size("front")
    layers = lax.axis_size("layer")
    members = devices // child_map.shape[0]
    group = devices // parent_map.shape[0]
    rows = child_rhs.shape[2]
    both = 2 * rows
    root_size = root_inverse.shape[1]
    parent_size = parent_inverse.shape[1]
    where = functools.partial(lax.axis_index, "front")
    layer = functools.partial(lax.axis_index, "layer")

    def trade(value, k):
        return lax.ppermute(value, "front", [(d, d ^ k) for d in range(devices)])

    rhs = child_rhs[0].reshape(both, child_rhs.shape[3])
    child_width = child_update.shape[2]
    parent_width = parent_update.shape[2]
    root_share = root_size // devices
    hbm = pl.BlockSpec(memory_space=pltpu.HBM)
    (inverse, update, partial, child_low, parent_low, columns, parent_columns, *masks) = pl.pallas_call(
        functools.partial(load_kernel, members, group, where, layer),
        name="load",
        out_shape=[
            jax.ShapeDtypeStruct(shape, dtype)
            for shape, dtype in (
                (child_inverse.shape[1:], BF),
                (child_update.shape[1:], BF),
                ((both, child_inverse.shape[2]), F32),
                ((LOW, child_width), BF),
                ((LOW, parent_width), BF),
                ((1, child_width), jnp.int32),
                ((1, parent_width), jnp.int32),
                ((both, 2 * root_share), F32),
                ((1, 2 * root_share), F32),
                ((1, root_share), F32),
                ((1, root_share), F32),
            )
        ],
        in_specs=[hbm] * 6,
        out_specs=[WHOLE] * 11,
        scratch_shapes=[
            pltpu.VMEM(rhs.shape, BF),
            pltpu.VMEM(child_map.shape, jnp.int32),
            pltpu.VMEM(parent_map.shape, jnp.int32),
            pltpu.VMEM((both, root_share), BF),
            pltpu.SemaphoreType.DMA((6,)),
        ],
        compiler_params=pltpu.CompilerParams(vmem_limit_bytes=8 << 20),
        cost_estimate=pl.CostEstimate(
            flops=both * child_inverse.size, bytes_accessed=child_inverse.size * 8, transcendentals=0
        ),
    )(
        *[
            pltpu.with_memory_space_constraint(value, pltpu.HBM)
            for value in (
                child_inverse[0],
                child_update[0],
                rhs,
                child_map,
                parent_map,
                root_rhs[0].reshape(both, root_share),
            )
        ]
    )
    placed_rhs, keep, lower_in, upper_in = masks
    share = parent_size // group
    *sends, terms = call(
        functools.partial(child_kernel, members - 1, members, group, where),
        "child",
        [((both, share), BF)] * group + [((both, child_width), BF)],
        [pltpu.VMEM((4 * both, child_width), BF), pltpu.VMEM((both, parent_size), BF)],
        8 << 20,
        (both * 2 * child_inverse.size * 2, child_inverse.size * 4),
        *[trade(rhs, k) for k in range(1, members)],
        partial,
        inverse,
        update,
        columns,
        child_low,
    )
    (child_root,) = call(
        functools.partial(child_root_kernel, parent_size // LOW),
        "child_root",
        [((both, root_size), BF)],
        [pltpu.VMEM((4 * both, child_width), BF)],
        8 << 20,
        (both * 2 * root_size * child_width, root_size * both * 4),
        terms,
        columns,
        child_low,
    )
    summed = sends[0].astype(F32)
    for k in range(1, group):
        summed = summed + trade(sends[k], k).astype(F32)
    parent_now = (
        parent_rhs[0].reshape(both, parent_rhs.shape[3]).astype(F32) - summed
    ).astype(BF)
    pieces = [parent_now] + [trade(parent_now, k) for k in range(1, group)]
    sends = call(
        functools.partial(parent_kernel, group, where),
        "parent",
        [((rows, 2 * root_share), BF)] * (2 * group),
        [
            pltpu.VMEM((both, parent_width), BF),
            pltpu.VMEM((4 * both, parent_width), BF),
            pltpu.VMEM((both, root_size), BF),
        ],
        14 << 20,
        (both * 2 * root_size * parent_width, parent_update.size * 4),
        *pieces,
        parent_inverse[0],
        parent_update[0],
        parent_columns,
        parent_low,
        child_root,
    )

    def group_sum(parts, block):
        total = parts[0].astype(F32)
        for k in range(1, group):
            total = total + trade(parts[k], k).astype(F32)
        return total - placed_rhs[block * rows : (block + 1) * rows]

    def gathered(now):
        return [now] + [trade(now, k) for k in range(1, group)]

    def crossed(part, narrow):
        return part + trade(narrow, group).astype(F32)

    root_cost = (rows * 2 * root_inverse.size, root_inverse.size * 2)
    part = group_sum(sends[:group], 0)
    narrow, *second_sends = lax.optimization_barrier((part.astype(BF), *sends[group:]))
    total = crossed(part, narrow)
    now = -total * keep
    first_sol, outgoing = call(
        functools.partial(first_root_kernel, group, where),
        "root_first",
        [((rows, root_share), BF), ((rows, root_share), BF)],
        [],
        4 << 20,
        root_cost,
        *gathered(now.astype(BF)),
        root_inverse[0],
        coupling,
    )
    places = [(one, d) for one in range(layers) for d in range(devices)]
    same = [(g * devices + d, (g + 1) % layers * devices + d) for g, d in places]
    over = [(g * devices + d, (g + 1) % layers * devices + (d ^ group)) for g, d in places]
    incoming = lax.ppermute(outgoing, ("layer", "front"), same).astype(F32)
    beside = lax.ppermute(outgoing, ("layer", "front"), over).astype(F32)
    part = group_sum(second_sends, 1)
    total = crossed(part, part.astype(BF))
    arrived = jnp.concatenate([incoming * lower_in + beside * upper_in, incoming * upper_in], 1)
    now = -(total + arrived) * keep
    (out,) = call(
        functools.partial(second_root_kernel, group, where),
        "root_second",
        [((both, root_share), BF)],
        [],
        4 << 20,
        root_cost,
        *gathered(now.astype(BF)),
        root_inverse[0],
        first_sol,
    )
    return out.reshape(1, 2, rows, root_share)


def solution(mesh):
    placed = (
        P("layer", None, None, "front"),
        P("layer", None, None, "front"),
        P("layer", None, None, "front"),
        P("layer", None, "front"),
        P("layer", "front", None),
        P("layer", None, "front"),
        P("layer", "front", None),
        P("layer", None, "front"),
        P("layer", "front"),
        P(),
        P(),
    )
    return jax.shard_map(
        body, mesh=mesh, in_specs=placed, out_specs=P("layer", None, None, "front"), check_vma=False
    )
```

```python
import functools

import jax
import jax.numpy as jnp
from jax import lax
from jax.experimental import pallas as pl
from jax.experimental.pallas import tpu as pltpu
from jax.sharding import PartitionSpec as P


LOW = 256
BF = jnp.bfloat16
F32 = jnp.float32
WHOLE = pl.BlockSpec(memory_space=pltpu.VMEM)


def call(kernel, outs, scratch, limit, cost, *args):
    return pl.pallas_call(
        kernel,
        out_shape=[jax.ShapeDtypeStruct(shape, dtype) for shape, dtype in outs],
        in_specs=[WHOLE] * len(args),
        out_specs=[WHOLE] * len(outs),
        scratch_shapes=scratch,
        compiler_params=pltpu.CompilerParams(vmem_limit_bytes=limit),
        cost_estimate=pl.CostEstimate(flops=cost[0], bytes_accessed=cost[1], transcendentals=0),
    )(*args)


def one_hot_rows(columns, low_ref):
    width = columns.shape[1]
    lane = lax.broadcasted_iota(jnp.int32, (LOW, width), 0)
    low_ref[...] = jnp.where(lane == (columns & (LOW - 1)), 1.0, 0.0).astype(BF)


def place_columns(values, columns, first, blocks, low_ref, stack_ref, put):
    rows = values.shape[0]
    high = columns // LOW
    together = stack_ref.shape[0] // rows
    for start in range(0, blocks, together):
        count = min(together, blocks - start)
        for j in range(count):
            here = jnp.where(high == first + start + j, 1.0, 0.0).astype(BF)
            stack_ref[j * rows : (j + 1) * rows, :] = values * here
        placed = lax.dot_general(
            stack_ref[: count * rows, :],
            low_ref[...],
            (((1,), (1,)), ((), ())),
            preferred_element_type=F32,
        )
        for j in range(count):
            put(start + j, placed[j * rows : (j + 1) * rows])


def shared_dot(pieces, weights, position, width, offset=0):
    total = None
    for k, piece in enumerate(pieces):
        first = pl.multiple_of(offset + (position ^ k) * width, width)
        part = jnp.dot(piece, weights[pl.ds(first, width), :], preferred_element_type=F32)
        total = part if total is None else total + part
    return total


def load_kernel(members, group, where, layer, *refs):
    (inverse, update, rhs, child_maps, parent_maps, root_rhs) = refs[:6]
    (inverse_v, update_v, partial, child_low, parent_low, columns, parent_columns) = refs[6:13]
    (placed_rhs, keep, lower_in, upper_in) = refs[13:17]
    rhs_v, child_maps_v, parent_maps_v, root_rhs_v, sems = refs[17:]
    pairs = (
        (child_maps, child_maps_v),
        (parent_maps, parent_maps_v),
        (root_rhs, root_rhs_v),
        (rhs, rhs_v),
        (inverse, inverse_v),
        (update, update_v),
    )
    copies = [pltpu.make_async_copy(a, b, sems.at[i]) for i, (a, b) in enumerate(pairs)]
    for copy in copies:
        copy.start()
    device = where()
    upper = device >= group
    copies[0].wait()
    columns[...] = child_maps_v[pl.ds(device // members, 1), :]
    one_hot_rows(columns[...], child_low)
    copies[1].wait()
    parent_columns[...] = parent_maps_v[pl.ds(device // group, 1), :]
    one_hot_rows(parent_columns[...], parent_low)
    copies[2].wait()
    width = root_rhs.shape[1]
    value = root_rhs_v[...].astype(F32)
    placed_rhs[:, :width] = jnp.where(upper, 0.0, value)
    placed_rhs[:, width:] = jnp.where(upper, value, 0.0)
    keep[:, :width] = jnp.ones((1, width), F32)
    above = jnp.where(upper, 1.0, 0.0)
    inside = jnp.where(layer() > 0, 1.0, 0.0)
    keep[:, width:] = jnp.full((1, width), above, F32)
    lower_in[...] = jnp.full((1, width), inside * (1.0 - above), F32)
    upper_in[...] = jnp.full((1, width), inside * above, F32)
    copies[3].wait()
    copies[4].wait()
    depth = rhs.shape[1]
    own = pl.multiple_of((device % members) * depth, depth)
    partial[...] = jnp.dot(
        rhs_v[...], inverse_v[pl.ds(own, depth), :], preferred_element_type=F32
    )
    copies[5].wait()


def child_kernel(pieces, members, group, where, *refs):
    piece_refs = refs[:pieces]
    partial, inverse, update, columns, low = refs[pieces : pieces + 5]
    sends = refs[pieces + 5 : pieces + 5 + group]
    terms, stack, summed = refs[pieces + 5 + group :]
    device = where()
    place, member = device % members, device % group
    solved = partial[...]
    for k, piece in enumerate(piece_refs, 1):
        depth = piece.shape[1]
        first = pl.multiple_of((place ^ k) * depth, depth)
        solved = solved + jnp.dot(
            piece[...], inverse[pl.ds(first, depth), :], preferred_element_type=F32
        )
    solved = solved.astype(BF)
    for start in range(0, update.shape[1], 512):
        terms[:, start : start + 512] = jnp.dot(
            solved, update[:, start : start + 512], preferred_element_type=F32
        ).astype(BF)

    def put(block, value):
        summed[:, block * LOW : (block + 1) * LOW] = value.astype(BF)

    place_columns(terms[...], columns[...], 0, summed.shape[1] // LOW, low, stack, put)
    width = sends[0].shape[1]
    for k, send in enumerate(sends):
        send[...] = summed[:, pl.ds(pl.multiple_of((member ^ k) * width, width), width)]


def child_root_kernel(parent_blocks, terms, columns, low, placed_ref, stack):
    def put(block, value):
        placed_ref[:, block * LOW : (block + 1) * LOW] = value.astype(BF)

    place_columns(
        terms[...], columns[...], parent_blocks, placed_ref.shape[1] // LOW, low, stack, put
    )


def parent_kernel(group, base, where, *refs):
    piece_refs = refs[:group]
    inverse, update, columns, low, child_root = refs[group : group + 5]
    sends = refs[group + 5 : 2 * group + 5]
    terms, stack, total = refs[2 * group + 5 :]
    member = where() % group
    rows, width = sends[0].shape[0], sends[0].shape[1] // 2
    here = slice(base, base + rows)
    solved = shared_dot([r[here, :] for r in piece_refs], inverse, member, piece_refs[0].shape[1])
    solved = solved.astype(BF)
    for start in range(0, update.shape[1], 512):
        terms[:, start : start + 512] = jnp.dot(
            solved, update[:, start : start + 512], preferred_element_type=F32
        ).astype(BF)

    def put(block, value):
        place = slice(block * LOW, (block + 1) * LOW)
        total[:, place] = (value + child_root[here, place].astype(F32)).astype(BF)

    place_columns(terms[...], columns[...], 0, total.shape[1] // LOW, low, stack, put)
    half = total.shape[1] // 2
    for k in range(group):
        first = pl.multiple_of((member ^ k) * width, width)
        second = pl.multiple_of(half + (member ^ k) * width, width)
        sends[k][:, :width] = total[:, pl.ds(first, width)]
        sends[k][:, width:] = total[:, pl.ds(second, width)]


def root_dot(group, where, piece_refs, inverse):
    member = where() % group
    width = piece_refs[0].shape[1] // 2
    lower = shared_dot([r[:, :width] for r in piece_refs], inverse, member, width)
    upper = shared_dot(
        [r[:, width:] for r in piece_refs], inverse, member, width, inverse.shape[0] // 2
    )
    return lower + upper


def first_root_kernel(group, where, *refs):
    piece_refs, (inverse, coupling, solved_ref, hand_ref) = refs[:group], refs[group:]
    solved = root_dot(group, where, piece_refs, inverse)
    solved_ref[...] = solved.astype(BF)
    hand_ref[...] = (coupling[...] * solved).astype(BF)


def second_root_kernel(group, where, *refs):
    piece_refs, (inverse, first_ref, out_ref) = refs[:group], refs[group:]
    solved = root_dot(group, where, piece_refs, inverse)
    rows = first_ref.shape[0]
    out_ref[:rows, :] = first_ref[...]
    out_ref[rows:, :] = solved.astype(BF)


def body(
    child_rhs,
    parent_rhs,
    root_rhs,
    child_inverse,
    child_update,
    parent_inverse,
    parent_update,
    root_inverse,
    coupling,
    child_map,
    parent_map,
):
    devices = lax.axis_size("front")
    layers = lax.axis_size("layer")
    members = devices // child_map.shape[0]
    group = devices // parent_map.shape[0]
    rows = child_rhs.shape[2]
    both = 2 * rows
    root_size = root_inverse.shape[1]
    parent_size = parent_inverse.shape[1]
    where = functools.partial(lax.axis_index, "front")
    layer = functools.partial(lax.axis_index, "layer")

    def trade(value, k):
        return lax.ppermute(value, "front", [(d, d ^ k) for d in range(devices)])

    rhs = child_rhs[0].reshape(both, child_rhs.shape[3])
    child_width = child_update.shape[2]
    parent_width = parent_update.shape[2]
    root_share = root_size // devices
    hbm = pl.BlockSpec(memory_space=pltpu.HBM)
    (inverse, update, partial, child_low, parent_low, columns, parent_columns, *masks) = pl.pallas_call(
        functools.partial(load_kernel, members, group, where, layer),
        name="load",
        out_shape=[
            jax.ShapeDtypeStruct(shape, dtype)
            for shape, dtype in (
                (child_inverse.shape[1:], BF),
                (child_update.shape[1:], BF),
                ((both, child_inverse.shape[2]), F32),
                ((LOW, child_width), BF),
                ((LOW, parent_width), BF),
                ((1, child_width), jnp.int32),
                ((1, parent_width), jnp.int32),
                ((both, 2 * root_share), F32),
                ((1, 2 * root_share), F32),
                ((1, root_share), F32),
                ((1, root_share), F32),
            )
        ],
        in_specs=[hbm] * 6,
        out_specs=[WHOLE] * 11,
        scratch_shapes=[
            pltpu.VMEM(rhs.shape, BF),
            pltpu.VMEM(child_map.shape, jnp.int32),
            pltpu.VMEM(parent_map.shape, jnp.int32),
            pltpu.VMEM((both, root_share), BF),
            pltpu.SemaphoreType.DMA((6,)),
        ],
        compiler_params=pltpu.CompilerParams(vmem_limit_bytes=8 << 20),
        cost_estimate=pl.CostEstimate(
            flops=both * child_inverse.size, bytes_accessed=child_inverse.size * 8, transcendentals=0
        ),
    )(
        *[
            pltpu.with_memory_space_constraint(value, pltpu.HBM)
            for value in (
                child_inverse[0],
                child_update[0],
                rhs,
                child_map,
                parent_map,
                root_rhs[0].reshape(both, root_share),
            )
        ]
    )
    placed_rhs, keep, lower_in, upper_in = masks
    share = parent_size // group
    *sends, terms = call(
        functools.partial(child_kernel, members - 1, members, group, where),
        [((both, share), BF)] * group + [((both, child_width), BF)],
        [pltpu.VMEM((4 * both, child_width), BF), pltpu.VMEM((both, parent_size), BF)],
        8 << 20,
        (both * 2 * child_inverse.size * 2, child_inverse.size * 4),
        *[trade(rhs, k) for k in range(1, members)],
        partial,
        inverse,
        update,
        columns,
        child_low,
    )
    (child_root,) = call(
        functools.partial(child_root_kernel, parent_size // LOW),
        [((both, root_size), BF)],
        [pltpu.VMEM((4 * both, child_width), BF)],
        8 << 20,
        (both * 2 * root_size * child_width, root_size * both * 4),
        terms,
        columns,
        child_low,
    )
    summed = sends[0].astype(F32)
    for k in range(1, group):
        summed = summed + trade(sends[k], k).astype(F32)
    parent_now = (
        parent_rhs[0].reshape(both, parent_rhs.shape[3]).astype(F32) - summed
    ).astype(BF)
    pieces = [parent_now] + [trade(parent_now, k) for k in range(1, group)]

    def parent_sends(block):
        return call(
            functools.partial(parent_kernel, group, block * rows, where),
            [((rows, 2 * root_share), BF)] * group,
            [
                pltpu.VMEM((rows, parent_width), BF),
                pltpu.VMEM((8 * rows, parent_width), BF),
                pltpu.VMEM((rows, root_size), BF),
            ],
            8 << 20,
            (rows * 2 * root_size * parent_width, parent_update.size * 4),
            *pieces,
            parent_inverse[0],
            parent_update[0],
            parent_columns,
            parent_low,
            child_root,
        )

    def group_sum(parts, block, after=()):
        arrived = [trade(parts[k], k) for k in range(1, group)]
        *_, first, arrived = lax.optimization_barrier((*after, parts[0], arrived))
        total = first.astype(F32)
        for value in arrived:
            total = total + value.astype(F32)
        return total - placed_rhs[block * rows : (block + 1) * rows]

    def gathered(now):
        return [now] + [trade(now, k) for k in range(1, group)]

    def crossed(part, narrow):
        return part + trade(narrow, group).astype(F32)

    root_cost = (rows * 2 * root_inverse.size, root_inverse.size * 2)
    part = group_sum(parent_sends(0), 0)
    now = (-crossed(part, part.astype(BF)) * keep).astype(BF)
    part = group_sum(parent_sends(1), 1, (now,))
    total = crossed(part, part.astype(BF))
    first_sol, outgoing = call(
        functools.partial(first_root_kernel, group, where),
        [((rows, root_share), BF), ((rows, root_share), BF)],
        [],
        4 << 20,
        root_cost,
        *gathered(now),
        root_inverse[0],
        coupling,
    )
    places = [(one, d) for one in range(layers) for d in range(devices)]
    same = [(g * devices + d, (g + 1) % layers * devices + d) for g, d in places]
    over = [(g * devices + d, (g + 1) % layers * devices + (d ^ group)) for g, d in places]
    incoming = lax.ppermute(outgoing, ("layer", "front"), same).astype(F32)
    beside = lax.ppermute(outgoing, ("layer", "front"), over).astype(F32)
    arrived = jnp.concatenate([incoming * lower_in + beside * upper_in, incoming * upper_in], 1)
    now = -(total + arrived) * keep
    (out,) = call(
        functools.partial(second_root_kernel, group, where),
        [((both, root_share), BF)],
        [],
        4 << 20,
        root_cost,
        *gathered(now.astype(BF)),
        root_inverse[0],
        first_sol,
    )
    return out.reshape(1, 2, rows, root_share)


def solution(mesh):
    placed = (
        P("layer", None, None, "front"),
        P("layer", None, None, "front"),
        P("layer", None, None, "front"),
        P("layer", None, "front"),
        P("layer", "front", None),
        P("layer", None, "front"),
        P("layer", "front", None),
        P("layer", None, "front"),
        P("layer", "front"),
        P(),
        P(),
    )

    return jax.shard_map(
        body, mesh=mesh, in_specs=placed, out_specs=P("layer", None, None, "front"), check_vma=False
    )
```

```python
import functools

import jax
import jax.numpy as jnp
from jax import lax
from jax.experimental import pallas as pl
from jax.experimental.pallas import tpu as pltpu
from jax.sharding import PartitionSpec as P


LOW = 256
BF = jnp.bfloat16
F32 = jnp.float32
WHOLE = pl.BlockSpec(memory_space=pltpu.VMEM)


def call(kernel, outs, scratch, limit, cost, *args):
    return pl.pallas_call(
        kernel,
        out_shape=[jax.ShapeDtypeStruct(shape, dtype) for shape, dtype in outs],
        in_specs=[WHOLE] * len(args),
        out_specs=[WHOLE] * len(outs),
        scratch_shapes=scratch,
        compiler_params=pltpu.CompilerParams(vmem_limit_bytes=limit),
        cost_estimate=pl.CostEstimate(flops=cost[0], bytes_accessed=cost[1], transcendentals=0),
    )(*args)


def one_hot_rows(columns, low_ref):
    width = columns.shape[1]
    lane = lax.broadcasted_iota(jnp.int32, (LOW, width), 0)
    low_ref[...] = jnp.where(lane == (columns & (LOW - 1)), 1.0, 0.0).astype(BF)


def place_columns(values, columns, first, blocks, low_ref, stack_ref, put):
    rows = values.shape[0]
    high = columns // LOW
    together = stack_ref.shape[0] // rows
    for start in range(0, blocks, together):
        count = min(together, blocks - start)
        for j in range(count):
            here = jnp.where(high == first + start + j, 1.0, 0.0).astype(BF)
            stack_ref[j * rows : (j + 1) * rows, :] = values * here
        placed = lax.dot_general(
            stack_ref[: count * rows, :],
            low_ref[...],
            (((1,), (1,)), ((), ())),
            preferred_element_type=F32,
        )
        for j in range(count):
            put(start + j, placed[j * rows : (j + 1) * rows])


def load_kernel(members, group, where, layer, *refs):
    (inverse, update, rhs, child_maps, parent_maps, root_rhs) = refs[:6]
    (inverse_v, update_v, partial, child_low, parent_low, columns, parent_columns) = refs[6:13]
    (placed_rhs, keep, lower_in, upper_in) = refs[13:17]
    rhs_v, child_maps_v, parent_maps_v, root_rhs_v, sems = refs[17:]
    pairs = (
        (child_maps, child_maps_v),
        (parent_maps, parent_maps_v),
        (root_rhs, root_rhs_v),
        (rhs, rhs_v),
        (inverse, inverse_v),
        (update, update_v),
    )
    copies = [pltpu.make_async_copy(a, b, sems.at[i]) for i, (a, b) in enumerate(pairs)]
    for copy in copies:
        copy.start()
    device = where()
    upper = device >= group
    copies[0].wait()
    columns[...] = child_maps_v[pl.ds(device // members, 1), :]
    one_hot_rows(columns[...], child_low)
    copies[1].wait()
    parent_columns[...] = parent_maps_v[pl.ds(device // group, 1), :]
    one_hot_rows(parent_columns[...], parent_low)
    copies[2].wait()
    width = root_rhs.shape[1]
    value = root_rhs_v[...].astype(F32)
    placed_rhs[:, :width] = jnp.where(upper, 0.0, value)
    placed_rhs[:, width:] = jnp.where(upper, value, 0.0)
    keep[:, :width] = jnp.ones((1, width), F32)
    above = jnp.where(upper, 1.0, 0.0)
    inside = jnp.where(layer() > 0, 1.0, 0.0)
    keep[:, width:] = jnp.full((1, width), above, F32)
    lower_in[...] = jnp.full((1, width), inside * (1.0 - above), F32)
    upper_in[...] = jnp.full((1, width), inside * above, F32)
    copies[3].wait()
    copies[4].wait()
    depth = rhs.shape[1]
    own = pl.multiple_of((device % members) * depth, depth)
    partial[...] = jnp.dot(
        rhs_v[...], inverse_v[pl.ds(own, depth), :], preferred_element_type=F32
    )
    copies[5].wait()


def child_kernel(pieces, base, members, group, where, *refs):
    piece_refs = refs[:pieces]
    partial, inverse, update, columns, low, rhs = refs[pieces : pieces + 6]
    out, terms, stack, summed = refs[pieces + 6 :]
    device = where()
    place, member = device % members, device % group
    here = slice(base, base + out.shape[0])
    solved = partial[here, :]
    for k, piece in enumerate(piece_refs, 1):
        depth = piece.shape[1]
        first = pl.multiple_of((place ^ k) * depth, depth)
        solved = solved + jnp.dot(
            piece[here, :], inverse[pl.ds(first, depth), :], preferred_element_type=F32
        )
    solved = solved.astype(BF)
    for start in range(0, update.shape[1], 512):
        terms[:, start : start + 512] = jnp.dot(
            solved, update[:, start : start + 512], preferred_element_type=F32
        ).astype(BF)

    def put(block, value):
        summed[:, block * LOW : (block + 1) * LOW] = value

    place_columns(terms[...], columns[...], 0, summed.shape[1] // LOW, low, stack, put)
    width = rhs.shape[1]
    own = pl.ds(pl.multiple_of(member * width, width), width)
    summed[:, own] = summed[:, own] - rhs[here, :].astype(F32)
    out[...] = summed[...].astype(BF)


def child_root_kernel(parent_blocks, terms, columns, low, placed_ref, stack):
    def put(block, value):
        placed_ref[:, block * LOW : (block + 1) * LOW] = value.astype(BF)

    place_columns(
        terms[...], columns[...], parent_blocks, placed_ref.shape[1] // LOW, low, stack, put
    )


def parent_kernel(group, where, *refs):
    now, inverse, update, columns, low, child_root = refs[:6]
    sends = refs[6 : 6 + group]
    terms, stack, total = refs[6 + group :]
    member = where() % group
    width = sends[0].shape[1] // 2
    solved = jnp.dot(now[...], inverse[...], preferred_element_type=F32).astype(BF)
    for start in range(0, update.shape[1], 512):
        terms[:, start : start + 512] = jnp.dot(
            solved, update[:, start : start + 512], preferred_element_type=F32
        ).astype(BF)

    def put(block, value):
        place = slice(block * LOW, (block + 1) * LOW)
        total[:, place] = (value + child_root[:, place].astype(F32)).astype(BF)

    place_columns(terms[...], columns[...], 0, total.shape[1] // LOW, low, stack, put)
    half = total.shape[1] // 2
    for k in range(group):
        first = pl.multiple_of((member ^ k) * width, width)
        second = pl.multiple_of(half + (member ^ k) * width, width)
        sends[k][:, :width] = total[:, pl.ds(first, width)]
        sends[k][:, width:] = total[:, pl.ds(second, width)]


def root_dot(group, where, members, piece_refs, inverse):
    member = where() % group
    half = inverse.shape[0] // 2
    total = None
    for k, piece in zip(members, piece_refs):
        width = piece.shape[1] // 2
        for part in range(2):
            first = pl.multiple_of(part * half + (member ^ k) * width, width)
            value = jnp.dot(
                piece[:, part * width : (part + 1) * width],
                inverse[pl.ds(first, width), :],
                preferred_element_type=F32,
            )
            total = value if total is None else total + value
    return total


def early_root_kernel(group, where, members, *refs):
    *piece_refs, inverse, total = refs
    total[...] = root_dot(group, where, members, piece_refs, inverse)


def first_root_kernel(group, where, members, *refs):
    *piece_refs, inverse, early, coupling, solved_ref, hand_ref = refs
    solved = early[...] + root_dot(group, where, members, piece_refs, inverse)
    solved_ref[...] = solved.astype(BF)
    hand_ref[...] = (coupling[...] * solved).astype(BF)


def second_root_kernel(group, where, members, *refs):
    *piece_refs, inverse, early, first_ref, out_ref = refs
    solved = early[...] + root_dot(group, where, members, piece_refs, inverse)
    rows = first_ref.shape[0]
    out_ref[:rows, :] = first_ref[...]
    out_ref[rows:, :] = solved.astype(BF)


def body(
    child_rhs,
    parent_rhs,
    root_rhs,
    child_inverse,
    child_update,
    parent_inverse,
    parent_update,
    root_inverse,
    coupling,
    child_map,
    parent_map,
):
    devices = lax.axis_size("front")
    layers = lax.axis_size("layer")
    members = devices // child_map.shape[0]
    group = devices // parent_map.shape[0]
    rows = child_rhs.shape[2]
    both = 2 * rows
    root_size = root_inverse.shape[1]
    parent_size = parent_inverse.shape[1]
    where = functools.partial(lax.axis_index, "front")
    layer = functools.partial(lax.axis_index, "layer")

    def trade(value, k):
        return lax.ppermute(value, "front", [(d, d ^ k) for d in range(devices)])

    rhs = child_rhs[0].reshape(both, child_rhs.shape[3])
    child_width = child_update.shape[2]
    parent_width = parent_update.shape[2]
    root_share = root_size // devices
    hbm = pl.BlockSpec(memory_space=pltpu.HBM)
    (inverse, update, partial, child_low, parent_low, columns, parent_columns, *masks) = pl.pallas_call(
        functools.partial(load_kernel, members, group, where, layer),
        name="load",
        out_shape=[
            jax.ShapeDtypeStruct(shape, dtype)
            for shape, dtype in (
                (child_inverse.shape[1:], BF),
                (child_update.shape[1:], BF),
                ((both, child_inverse.shape[2]), F32),
                ((LOW, child_width), BF),
                ((LOW, parent_width), BF),
                ((1, child_width), jnp.int32),
                ((1, parent_width), jnp.int32),
                ((both, 2 * root_share), F32),
                ((1, 2 * root_share), F32),
                ((1, root_share), F32),
                ((1, root_share), F32),
            )
        ],
        in_specs=[hbm] * 6,
        out_specs=[WHOLE] * 11,
        scratch_shapes=[
            pltpu.VMEM(rhs.shape, BF),
            pltpu.VMEM(child_map.shape, jnp.int32),
            pltpu.VMEM(parent_map.shape, jnp.int32),
            pltpu.VMEM((both, root_share), BF),
            pltpu.SemaphoreType.DMA((6,)),
        ],
        compiler_params=pltpu.CompilerParams(vmem_limit_bytes=8 << 20),
        cost_estimate=pl.CostEstimate(
            flops=both * child_inverse.size, bytes_accessed=child_inverse.size * 8, transcendentals=0
        ),
    )(
        *[
            pltpu.with_memory_space_constraint(value, pltpu.HBM)
            for value in (
                child_inverse[0],
                child_update[0],
                rhs,
                child_map,
                parent_map,
                root_rhs[0].reshape(both, root_share),
            )
        ]
    )
    placed_rhs, keep, lower_in, upper_in = masks
    own_rhs = parent_rhs[0].reshape(both, parent_rhs.shape[3])

    pieces = [trade(rhs, k) for k in range(1, members)]

    def child_part(block):
        return call(
            functools.partial(child_kernel, members - 1, block * rows, members, group, where),
            [((rows, parent_size), BF), ((rows, child_width), BF)],
            [pltpu.VMEM((8 * rows, child_width), BF), pltpu.VMEM((rows, parent_size), F32)],
            8 << 20,
            (rows * 2 * child_inverse.size * 2, child_inverse.size * 4),
            *pieces,
            partial,
            inverse,
            update,
            columns,
            child_low,
            own_rhs,
        )

    def parent_sends(block):
        part, terms = child_part(block)
        (child_root,) = call(
            functools.partial(child_root_kernel, parent_size // LOW),
            [((rows, root_size), BF)],
            [pltpu.VMEM((8 * rows, child_width), BF)],
            8 << 20,
            (rows * 2 * root_size * child_width, root_size * rows * 4),
            terms,
            columns,
            child_low,
        )
        steps = [1 << bit for bit in range((group - 1).bit_length())]
        for step in reversed(steps) if block else steps:
            part = (part.astype(F32) + trade(part, step).astype(F32)).astype(BF)
        return call(
            functools.partial(parent_kernel, group, where),
            [((rows, 2 * root_share), BF)] * group,
            [
                pltpu.VMEM((rows, parent_width), BF),
                pltpu.VMEM((8 * rows, parent_width), BF),
                pltpu.VMEM((rows, root_size), BF),
            ],
            8 << 20,
            (rows * 2 * root_size * parent_width, parent_update.size * 4),
            -part,
            parent_inverse[0],
            parent_update[0],
            parent_columns,
            parent_low,
            child_root,
        )

    def group_sum(parts, block, after=()):
        arrived = [trade(parts[k], k) for k in range(1, group)]
        own = parts[0]
        if after:
            *_, own = lax.optimization_barrier((*after, own))
        total = own.astype(F32) - placed_rhs[block * rows : (block + 1) * rows]
        if after:
            total, arrived = lax.optimization_barrier((total, arrived))
        for value in arrived:
            total = total + value.astype(F32)
        return total

    early_ones = (0, group - 1)
    late_ones = tuple(range(1, group - 1))

    def gathered(now):
        pieces = [now] + [trade(now, k) for k in range(1, group)]
        (early,) = call(
            functools.partial(early_root_kernel, group, where, early_ones),
            [((rows, root_share), F32)],
            [],
            4 << 20,
            root_cost,
            *[pieces[k] for k in early_ones],
            root_inverse[0],
        )
        return [pieces[k] for k in late_ones] + [root_inverse[0], early]

    def crossed(part, narrow):
        return part + trade(narrow, group).astype(F32)

    root_cost = (rows * root_inverse.size, root_inverse.size)
    part = group_sum(parent_sends(0), 0)
    now = (-crossed(part, part.astype(BF)) * keep).astype(BF)
    part = group_sum(parent_sends(1), 1, (now,))
    total = crossed(part, part.astype(BF))
    first_sol, outgoing = call(
        functools.partial(first_root_kernel, group, where, late_ones),
        [((rows, root_share), BF), ((rows, root_share), BF)],
        [],
        4 << 20,
        root_cost,
        *gathered(now),
        coupling,
    )
    places = [(one, d) for one in range(layers) for d in range(devices)]
    same = [(g * devices + d, (g + 1) % layers * devices + d) for g, d in places]
    over = [(g * devices + d, (g + 1) % layers * devices + (d ^ group)) for g, d in places]
    incoming = lax.ppermute(outgoing, ("layer", "front"), same).astype(F32)
    beside = lax.ppermute(outgoing, ("layer", "front"), over).astype(F32)
    arrived = jnp.concatenate([incoming * lower_in + beside * upper_in, incoming * upper_in], 1)
    now = -(total + arrived) * keep
    (out,) = call(
        functools.partial(second_root_kernel, group, where, late_ones),
        [((both, root_share), BF)],
        [],
        4 << 20,
        root_cost,
        *gathered(now.astype(BF)),
        first_sol,
    )
    return out.reshape(1, 2, rows, root_share)


def solution(mesh):
    placed = (
        P("layer", None, None, "front"),
        P("layer", None, None, "front"),
        P("layer", None, None, "front"),
        P("layer", None, "front"),
        P("layer", "front", None),
        P("layer", None, "front"),
        P("layer", "front", None),
        P("layer", None, "front"),
        P("layer", "front"),
        P(),
        P(),
    )

    return jax.shard_map(
        body, mesh=mesh, in_specs=placed, out_specs=P("layer", None, None, "front"), check_vma=False
    )
```

```python
import functools

import jax
import jax.numpy as jnp
from jax import lax
from jax.experimental import pallas as pl
from jax.experimental.pallas import tpu as pltpu
from jax.sharding import PartitionSpec as P


LOW = 256
BF = jnp.bfloat16
F32 = jnp.float32
WHOLE = pl.BlockSpec(memory_space=pltpu.VMEM)


def call(kernel, outs, scratch, limit, cost, *args):
    return pl.pallas_call(
        kernel,
        out_shape=[jax.ShapeDtypeStruct(shape, dtype) for shape, dtype in outs],
        in_specs=[WHOLE] * len(args),
        out_specs=[WHOLE] * len(outs),
        scratch_shapes=scratch,
        compiler_params=pltpu.CompilerParams(vmem_limit_bytes=limit),
        cost_estimate=pl.CostEstimate(flops=cost[0], bytes_accessed=cost[1], transcendentals=0),
    )(*args)


def one_hot_rows(columns, low_ref):
    width = columns.shape[1]
    lane = lax.broadcasted_iota(jnp.int32, (LOW, width), 0)
    low_ref[...] = jnp.where(lane == (columns & (LOW - 1)), 1.0, 0.0).astype(BF)


def place_columns(values, columns, first, blocks, low_ref, stack_ref, put):
    rows = values.shape[0]
    high = columns // LOW
    together = stack_ref.shape[0] // rows
    for start in range(0, blocks, together):
        count = min(together, blocks - start)
        for j in range(count):
            here = jnp.where(high == first + start + j, 1.0, 0.0).astype(BF)
            stack_ref[j * rows : (j + 1) * rows, :] = values * here
        placed = lax.dot_general(
            stack_ref[: count * rows, :],
            low_ref[...],
            (((1,), (1,)), ((), ())),
            preferred_element_type=F32,
        )
        for j in range(count):
            put(start + j, placed[j * rows : (j + 1) * rows])


def load_kernel(members, group, where, layer, *refs):
    (inverse, rhs, child_maps, parent_maps, root_rhs) = refs[:5]
    (inverse_v, partial, child_low, parent_low, columns, parent_columns) = refs[5:11]
    (placed_rhs, keep, lower_in, upper_in) = refs[11:15]
    rhs_v, child_maps_v, parent_maps_v, root_rhs_v, sems = refs[15:]
    pairs = (
        (child_maps, child_maps_v),
        (parent_maps, parent_maps_v),
        (root_rhs, root_rhs_v),
        (rhs, rhs_v),
        (inverse, inverse_v),
    )
    copies = [pltpu.make_async_copy(a, b, sems.at[i]) for i, (a, b) in enumerate(pairs)]
    for copy in copies:
        copy.start()
    device = where()
    upper = device >= group
    copies[0].wait()
    columns[...] = child_maps_v[pl.ds(device // members, 1), :]
    one_hot_rows(columns[...], child_low)
    copies[1].wait()
    parent_columns[...] = parent_maps_v[pl.ds(device // group, 1), :]
    one_hot_rows(parent_columns[...], parent_low)
    copies[2].wait()
    width = root_rhs.shape[1]
    value = root_rhs_v[...].astype(F32)
    placed_rhs[:, :width] = jnp.where(upper, 0.0, value)
    placed_rhs[:, width:] = jnp.where(upper, value, 0.0)
    keep[:, :width] = jnp.ones((1, width), F32)
    above = jnp.where(upper, 1.0, 0.0)
    inside = jnp.where(layer() > 0, 1.0, 0.0)
    keep[:, width:] = jnp.full((1, width), above, F32)
    lower_in[...] = jnp.full((1, width), inside * (1.0 - above), F32)
    upper_in[...] = jnp.full((1, width), inside * above, F32)
    copies[3].wait()
    copies[4].wait()
    depth = rhs.shape[1]
    own = pl.multiple_of((device % members) * depth, depth)
    partial[...] = jnp.dot(
        rhs_v[...], inverse_v[pl.ds(own, depth), :], preferred_element_type=F32
    )


def child_kernel(pieces, base, members, group, where, *refs):
    piece_refs = refs[:pieces]
    partial, inverse, update, columns, low, rhs = refs[pieces : pieces + 6]
    out, terms, stack, summed = refs[pieces + 6 :]
    device = where()
    place, member = device % members, device % group
    here = slice(base, base + out.shape[0])
    solved = partial[here, :]
    for k, piece in enumerate(piece_refs, 1):
        depth = piece.shape[1]
        first = pl.multiple_of((place ^ k) * depth, depth)
        solved = solved + jnp.dot(
            piece[...], inverse[pl.ds(first, depth), :], preferred_element_type=F32
        )
    solved = solved.astype(BF)
    for start in range(0, update.shape[1], 512):
        terms[:, start : start + 512] = jnp.dot(
            solved, update[:, start : start + 512], preferred_element_type=F32
        ).astype(BF)

    def put(block, value):
        summed[:, block * LOW : (block + 1) * LOW] = value

    place_columns(terms[...], columns[...], 0, summed.shape[1] // LOW, low, stack, put)
    width = rhs.shape[1]
    own = pl.ds(pl.multiple_of(member * width, width), width)
    summed[:, own] = summed[:, own] - rhs[here, :].astype(F32)
    out[...] = summed[...].astype(BF)


def child_root_kernel(parent_blocks, terms, columns, low, placed_ref, stack):
    def put(block, value):
        placed_ref[:, block * LOW : (block + 1) * LOW] = value.astype(BF)

    place_columns(
        terms[...], columns[...], parent_blocks, placed_ref.shape[1] // LOW, low, stack, put
    )


def parent_kernel(group, where, *refs):
    now, inverse, update, columns, low, child_root = refs[:6]
    sends = refs[6 : 6 + group]
    terms, stack, total = refs[6 + group :]
    member = where() % group
    width = sends[0].shape[1] // 2
    solved = jnp.dot(now[...], inverse[...], preferred_element_type=F32).astype(BF)
    for start in range(0, update.shape[1], 512):
        terms[:, start : start + 512] = jnp.dot(
            solved, update[:, start : start + 512], preferred_element_type=F32
        ).astype(BF)

    def put(block, value):
        place = slice(block * LOW, (block + 1) * LOW)
        total[:, place] = (value + child_root[:, place].astype(F32)).astype(BF)

    place_columns(terms[...], columns[...], 0, total.shape[1] // LOW, low, stack, put)
    half = total.shape[1] // 2
    for k in range(group):
        first = pl.multiple_of((member ^ k) * width, width)
        second = pl.multiple_of(half + (member ^ k) * width, width)
        sends[k][:, :width] = total[:, pl.ds(first, width)]
        sends[k][:, width:] = total[:, pl.ds(second, width)]


def root_dot(group, where, members, piece_refs, inverse):
    member = where() % group
    half = inverse.shape[0] // 2
    total = None
    for k, piece in zip(members, piece_refs):
        width = piece.shape[1] // 2
        for part in range(2):
            first = pl.multiple_of(part * half + (member ^ k) * width, width)
            value = jnp.dot(
                piece[:, part * width : (part + 1) * width],
                inverse[pl.ds(first, width), :],
                preferred_element_type=F32,
            )
            total = value if total is None else total + value
    return total


def early_root_kernel(group, where, members, *refs):
    *piece_refs, inverse, total = refs
    total[...] = root_dot(group, where, members, piece_refs, inverse)


def first_root_kernel(group, where, members, *refs):
    *piece_refs, inverse, early, coupling, solved_ref, hand_ref = refs
    solved = early[...] + root_dot(group, where, members, piece_refs, inverse)
    solved_ref[...] = solved.astype(BF)
    hand_ref[...] = (coupling[...] * solved).astype(BF)


def second_root_kernel(group, where, members, *refs):
    *piece_refs, inverse, early, first_ref, out_ref = refs
    solved = early[...] + root_dot(group, where, members, piece_refs, inverse)
    rows = first_ref.shape[0]
    out_ref[:rows, :] = first_ref[...]
    out_ref[rows:, :] = solved.astype(BF)


def body(
    child_rhs,
    parent_rhs,
    root_rhs,
    child_inverse,
    child_update,
    parent_inverse,
    parent_update,
    root_inverse,
    coupling,
    child_map,
    parent_map,
):
    devices = lax.axis_size("front")
    layers = lax.axis_size("layer")
    members = devices // child_map.shape[0]
    group = devices // parent_map.shape[0]
    rows = child_rhs.shape[2]
    both = 2 * rows
    root_size = root_inverse.shape[1]
    parent_size = parent_inverse.shape[1]
    where = functools.partial(lax.axis_index, "front")
    layer = functools.partial(lax.axis_index, "layer")

    def trade(value, k):
        return lax.ppermute(value, "front", [(d, d ^ k) for d in range(devices)])

    rhs = child_rhs[0].reshape(both, child_rhs.shape[3])
    child_width = child_update.shape[2]
    parent_width = parent_update.shape[2]
    root_share = root_size // devices
    hbm = pl.BlockSpec(memory_space=pltpu.HBM)
    (inverse, partial, child_low, parent_low, columns, parent_columns, *masks) = pl.pallas_call(
        functools.partial(load_kernel, members, group, where, layer),
        name="load",
        out_shape=[
            jax.ShapeDtypeStruct(shape, dtype)
            for shape, dtype in (
                (child_inverse.shape[1:], BF),
                ((both, child_inverse.shape[2]), F32),
                ((LOW, child_width), BF),
                ((LOW, parent_width), BF),
                ((1, child_width), jnp.int32),
                ((1, parent_width), jnp.int32),
                ((both, 2 * root_share), F32),
                ((1, 2 * root_share), F32),
                ((1, root_share), F32),
                ((1, root_share), F32),
            )
        ],
        in_specs=[hbm] * 5,
        out_specs=[WHOLE] * 10,
        scratch_shapes=[
            pltpu.VMEM(rhs.shape, BF),
            pltpu.VMEM(child_map.shape, jnp.int32),
            pltpu.VMEM(parent_map.shape, jnp.int32),
            pltpu.VMEM((both, root_share), BF),
            pltpu.SemaphoreType.DMA((5,)),
        ],
        compiler_params=pltpu.CompilerParams(vmem_limit_bytes=8 << 20),
        cost_estimate=pl.CostEstimate(
            flops=both * child_inverse.size, bytes_accessed=child_inverse.size * 8, transcendentals=0
        ),
    )(
        *[
            pltpu.with_memory_space_constraint(value, pltpu.HBM)
            for value in (
                child_inverse[0],
                rhs,
                child_map,
                parent_map,
                root_rhs[0].reshape(both, root_share),
            )
        ]
    )
    placed_rhs, keep, lower_in, upper_in = masks
    own_rhs = parent_rhs[0].reshape(both, parent_rhs.shape[3])

    def child_part(block):
        return call(
            functools.partial(child_kernel, members - 1, block * rows, members, group, where),
            [((rows, parent_size), BF), ((rows, child_width), BF)],
            [pltpu.VMEM((8 * rows, child_width), BF), pltpu.VMEM((rows, parent_size), F32)],
            8 << 20,
            (rows * 2 * child_inverse.size * 2, child_inverse.size * 4),
            *[trade(rhs[block * rows : (block + 1) * rows], k) for k in range(1, members)],
            partial,
            inverse,
            child_update[0],
            columns,
            child_low,
            own_rhs,
        )

    def parent_sends(block):
        part, terms = child_part(block)
        (child_root,) = call(
            functools.partial(child_root_kernel, parent_size // LOW),
            [((rows, root_size), BF)],
            [pltpu.VMEM((8 * rows, child_width), BF)],
            8 << 20,
            (rows * 2 * root_size * child_width, root_size * rows * 4),
            terms,
            columns,
            child_low,
        )
        steps = [1 << bit for bit in range((group - 1).bit_length())]
        for step in reversed(steps) if block else steps:
            part = (part.astype(F32) + trade(part, step).astype(F32)).astype(BF)
        return call(
            functools.partial(parent_kernel, group, where),
            [((rows, 2 * root_share), BF)] * group,
            [
                pltpu.VMEM((rows, parent_width), BF),
                pltpu.VMEM((8 * rows, parent_width), BF),
                pltpu.VMEM((rows, root_size), BF),
            ],
            8 << 20,
            (rows * 2 * root_size * parent_width, parent_update.size * 4),
            -part,
            parent_inverse[0],
            parent_update[0],
            parent_columns,
            parent_low,
            child_root,
        )

    def group_sum(parts, block, after=()):
        arrived = [trade(parts[k], k) for k in range(1, group)]
        own = parts[0]
        if after:
            *_, own = lax.optimization_barrier((*after, own))
        total = own.astype(F32) - placed_rhs[block * rows : (block + 1) * rows]
        if after:
            total, arrived = lax.optimization_barrier((total, arrived))
        for value in arrived:
            total = total + value.astype(F32)
        return total

    early_ones = (0, *range(2, group))
    late_ones = (1,)

    def gathered(now):
        pieces = [now] + [trade(now, k) for k in range(1, group)]
        (early,) = call(
            functools.partial(early_root_kernel, group, where, early_ones),
            [((rows, root_share), F32)],
            [],
            4 << 20,
            root_cost,
            *[pieces[k] for k in early_ones],
            root_inverse[0],
        )
        return [pieces[k] for k in late_ones] + [root_inverse[0], early]

    def crossed(part, narrow):
        return part + trade(narrow, group).astype(F32)

    root_cost = (rows * root_inverse.size, root_inverse.size)
    part = group_sum(parent_sends(0), 0)
    now = (-crossed(part, part.astype(BF)) * keep).astype(BF)
    part = group_sum(parent_sends(1), 1, (now,))
    total = crossed(part, part.astype(BF))
    first_sol, outgoing = call(
        functools.partial(first_root_kernel, group, where, late_ones),
        [((rows, root_share), BF), ((rows, root_share), BF)],
        [],
        4 << 20,
        root_cost,
        *gathered(now),
        coupling,
    )
    places = [(one, d) for one in range(layers) for d in range(devices)]
    same = [(g * devices + d, (g + 1) % layers * devices + d) for g, d in places]
    over = [(g * devices + d, (g + 1) % layers * devices + (d ^ group)) for g, d in places]
    incoming = lax.ppermute(outgoing, ("layer", "front"), same).astype(F32)
    beside = lax.ppermute(outgoing, ("layer", "front"), over).astype(F32)
    arrived = jnp.concatenate([incoming * lower_in + beside * upper_in, incoming * upper_in], 1)
    now = -(total + arrived) * keep
    (out,) = call(
        functools.partial(second_root_kernel, group, where, late_ones),
        [((both, root_share), BF)],
        [],
        4 << 20,
        root_cost,
        *gathered(now.astype(BF)),
        first_sol,
    )
    return out.reshape(1, 2, rows, root_share)


def solution(mesh):
    placed = (
        P("layer", None, None, "front"),
        P("layer", None, None, "front"),
        P("layer", None, None, "front"),
        P("layer", None, "front"),
        P("layer", "front", None),
        P("layer", None, "front"),
        P("layer", "front", None),
        P("layer", None, "front"),
        P("layer", "front"),
        P(),
        P(),
    )

    return jax.shard_map(
        body, mesh=mesh, in_specs=placed, out_specs=P("layer", None, None, "front"), check_vma=False
    )
```

```python
import functools

import jax
import jax.numpy as jnp
from jax import lax
from jax.experimental import pallas as pl
from jax.experimental.pallas import tpu as pltpu
from jax.sharding import PartitionSpec as P


LOW = 256
BF = jnp.bfloat16
F32 = jnp.float32
WHOLE = pl.BlockSpec(memory_space=pltpu.VMEM)


def call(kernel, outs, scratch, limit, cost, *args):
    return pl.pallas_call(
        kernel,
        out_shape=[jax.ShapeDtypeStruct(shape, dtype) for shape, dtype in outs],
        in_specs=[WHOLE] * len(args),
        out_specs=[WHOLE] * len(outs),
        scratch_shapes=scratch,
        compiler_params=pltpu.CompilerParams(vmem_limit_bytes=limit),
        cost_estimate=pl.CostEstimate(flops=cost[0], bytes_accessed=cost[1], transcendentals=0),
    )(*args)


def one_hot_rows(columns, low_ref):
    width = columns.shape[1]
    lane = lax.broadcasted_iota(jnp.int32, (LOW, width), 0)
    low_ref[...] = jnp.where(lane == (columns & (LOW - 1)), 1.0, 0.0).astype(BF)


def place_columns(values, columns, first, blocks, low_ref, stack_ref, put):
    rows = values.shape[0]
    high = columns // LOW
    together = stack_ref.shape[0] // rows
    for start in range(0, blocks, together):
        count = min(together, blocks - start)
        for j in range(count):
            here = jnp.where(high == first + start + j, 1.0, 0.0).astype(BF)
            stack_ref[j * rows : (j + 1) * rows, :] = values * here
        placed = lax.dot_general(
            stack_ref[: count * rows, :],
            low_ref[...],
            (((1,), (1,)), ((), ())),
            preferred_element_type=F32,
        )
        for j in range(count):
            put(start + j, placed[j * rows : (j + 1) * rows])


def load_kernel(members, group, where, layer, *refs):
    (inverse, rhs, child_maps, parent_maps, root_rhs) = refs[:5]
    (inverse_v, partial, child_low, parent_low, columns, parent_columns) = refs[5:11]
    (placed_rhs, keep, lower_in, upper_in) = refs[11:15]
    rhs_v, child_maps_v, parent_maps_v, root_rhs_v, sems = refs[15:]
    pairs = (
        (child_maps, child_maps_v),
        (parent_maps, parent_maps_v),
        (root_rhs, root_rhs_v),
        (rhs, rhs_v),
        (inverse, inverse_v),
    )
    copies = [pltpu.make_async_copy(a, b, sems.at[i]) for i, (a, b) in enumerate(pairs)]
    for copy in copies:
        copy.start()
    device = where()
    upper = device >= group
    copies[0].wait()
    columns[...] = child_maps_v[pl.ds(device // members, 1), :]
    one_hot_rows(columns[...], child_low)
    copies[1].wait()
    parent_columns[...] = parent_maps_v[pl.ds(device // group, 1), :]
    one_hot_rows(parent_columns[...], parent_low)
    copies[2].wait()
    width = root_rhs.shape[1]
    value = root_rhs_v[...].astype(F32)
    placed_rhs[:, :width] = jnp.where(upper, 0.0, value)
    placed_rhs[:, width:] = jnp.where(upper, value, 0.0)
    keep[:, :width] = jnp.ones((1, width), F32)
    above = jnp.where(upper, 1.0, 0.0)
    inside = jnp.where(layer() > 0, 1.0, 0.0)
    keep[:, width:] = jnp.full((1, width), above, F32)
    lower_in[...] = jnp.full((1, width), inside * (1.0 - above), F32)
    upper_in[...] = jnp.full((1, width), inside * above, F32)
    copies[3].wait()
    copies[4].wait()
    depth = rhs.shape[1]
    own = pl.multiple_of((device % members) * depth, depth)
    partial[...] = jnp.dot(
        rhs_v[...], inverse_v[pl.ds(own, depth), :], preferred_element_type=F32
    )


def child_kernel(pieces, base, members, group, where, *refs):
    piece_refs = refs[:pieces]
    partial, inverse, update, columns, low, rhs = refs[pieces : pieces + 6]
    out, terms, stack, summed = refs[pieces + 6 :]
    device = where()
    place, member = device % members, device % group
    here = slice(base, base + out.shape[0])
    solved = partial[here, :]
    for k, piece in enumerate(piece_refs, 1):
        depth = piece.shape[1]
        first = pl.multiple_of((place ^ k) * depth, depth)
        solved = solved + jnp.dot(
            piece[...], inverse[pl.ds(first, depth), :], preferred_element_type=F32
        )
    solved = solved.astype(BF)
    for start in range(0, update.shape[1], 512):
        terms[:, start : start + 512] = jnp.dot(
            solved, update[:, start : start + 512], preferred_element_type=F32
        ).astype(BF)

    def put(block, value):
        summed[:, block * LOW : (block + 1) * LOW] = value

    place_columns(terms[...], columns[...], 0, summed.shape[1] // LOW, low, stack, put)
    width = rhs.shape[1]
    own = pl.ds(pl.multiple_of(member * width, width), width)
    summed[:, own] = summed[:, own] - rhs[here, :].astype(F32)
    out[...] = summed[...].astype(BF)


def child_root_kernel(parent_blocks, terms, columns, low, placed_ref, stack):
    def put(block, value):
        placed_ref[:, block * LOW : (block + 1) * LOW] = value.astype(BF)

    place_columns(
        terms[...], columns[...], parent_blocks, placed_ref.shape[1] // LOW, low, stack, put
    )


def parent_kernel(group, where, *refs):
    now, inverse, update, columns, low, child_root = refs[:6]
    sends = refs[6 : 6 + group]
    terms, stack, total = refs[6 + group :]
    member = where() % group
    width = sends[0].shape[1] // 2
    solved = jnp.dot(now[...], inverse[...], preferred_element_type=F32).astype(BF)
    for start in range(0, update.shape[1], 512):
        terms[:, start : start + 512] = jnp.dot(
            solved, update[:, start : start + 512], preferred_element_type=F32
        ).astype(BF)

    def put(block, value):
        place = slice(block * LOW, (block + 1) * LOW)
        total[:, place] = (value + child_root[:, place].astype(F32)).astype(BF)

    place_columns(terms[...], columns[...], 0, total.shape[1] // LOW, low, stack, put)
    half = total.shape[1] // 2
    for k in range(group):
        first = pl.multiple_of((member ^ k) * width, width)
        second = pl.multiple_of(half + (member ^ k) * width, width)
        sends[k][:, :width] = total[:, pl.ds(first, width)]
        sends[k][:, width:] = total[:, pl.ds(second, width)]


def root_dot(group, where, members, piece_refs, inverse):
    member = where() % group
    half = inverse.shape[0] // 2
    total = None
    for k, piece in zip(members, piece_refs):
        width = piece.shape[1] // 2
        for part in range(2):
            first = pl.multiple_of(part * half + (member ^ k) * width, width)
            value = jnp.dot(
                piece[:, part * width : (part + 1) * width],
                inverse[pl.ds(first, width), :],
                preferred_element_type=F32,
            )
            total = value if total is None else total + value
    return total


def early_root_kernel(group, where, members, *refs):
    *piece_refs, inverse, total = refs
    total[...] = root_dot(group, where, members, piece_refs, inverse)


def first_root_kernel(group, where, members, *refs):
    *piece_refs, inverse, early, coupling, solved_ref, hand_ref = refs
    solved = early[...] + root_dot(group, where, members, piece_refs, inverse)
    solved_ref[...] = solved.astype(BF)
    hand_ref[...] = (coupling[...] * solved).astype(BF)


def second_root_kernel(group, where, members, *refs):
    *piece_refs, inverse, early, first_ref, out_ref = refs
    solved = early[...] + root_dot(group, where, members, piece_refs, inverse)
    rows = first_ref.shape[0]
    out_ref[:rows, :] = first_ref[...]
    out_ref[rows:, :] = solved.astype(BF)


def body(
    child_rhs,
    parent_rhs,
    root_rhs,
    child_inverse,
    child_update,
    parent_inverse,
    parent_update,
    root_inverse,
    coupling,
    child_map,
    parent_map,
):
    devices = lax.axis_size("front")
    layers = lax.axis_size("layer")
    members = devices // child_map.shape[0]
    group = devices // parent_map.shape[0]
    rows = child_rhs.shape[2]
    both = 2 * rows
    root_size = root_inverse.shape[1]
    parent_size = parent_inverse.shape[1]
    where = functools.partial(lax.axis_index, "front")
    layer = functools.partial(lax.axis_index, "layer")

    def trade(value, k):
        return lax.ppermute(value, "front", [(d, d ^ k) for d in range(devices)])

    rhs = child_rhs[0].reshape(both, child_rhs.shape[3])
    child_width = child_update.shape[2]
    parent_width = parent_update.shape[2]
    root_share = root_size // devices
    hbm = pl.BlockSpec(memory_space=pltpu.HBM)
    (inverse, partial, child_low, parent_low, columns, parent_columns, *masks) = pl.pallas_call(
        functools.partial(load_kernel, members, group, where, layer),
        name="load",
        out_shape=[
            jax.ShapeDtypeStruct(shape, dtype)
            for shape, dtype in (
                (child_inverse.shape[1:], BF),
                ((both, child_inverse.shape[2]), F32),
                ((LOW, child_width), BF),
                ((LOW, parent_width), BF),
                ((1, child_width), jnp.int32),
                ((1, parent_width), jnp.int32),
                ((both, 2 * root_share), F32),
                ((1, 2 * root_share), F32),
                ((1, root_share), F32),
                ((1, root_share), F32),
            )
        ],
        in_specs=[hbm] * 5,
        out_specs=[WHOLE] * 10,
        scratch_shapes=[
            pltpu.VMEM(rhs.shape, BF),
            pltpu.VMEM(child_map.shape, jnp.int32),
            pltpu.VMEM(parent_map.shape, jnp.int32),
            pltpu.VMEM((both, root_share), BF),
            pltpu.SemaphoreType.DMA((5,)),
        ],
        compiler_params=pltpu.CompilerParams(vmem_limit_bytes=8 << 20),
        cost_estimate=pl.CostEstimate(
            flops=both * child_inverse.size, bytes_accessed=child_inverse.size * 8, transcendentals=0
        ),
    )(
        *[
            pltpu.with_memory_space_constraint(value, pltpu.HBM)
            for value in (
                child_inverse[0],
                rhs,
                child_map,
                parent_map,
                root_rhs[0].reshape(both, root_share),
            )
        ]
    )
    placed_rhs, keep, lower_in, upper_in = masks
    own_rhs = parent_rhs[0].reshape(both, parent_rhs.shape[3])

    def child_part(block):
        return call(
            functools.partial(child_kernel, members - 1, block * rows, members, group, where),
            [((rows, parent_size), BF), ((rows, child_width), BF)],
            [pltpu.VMEM((8 * rows, child_width), BF), pltpu.VMEM((rows, parent_size), F32)],
            8 << 20,
            (rows * 2 * child_inverse.size * 2, child_inverse.size * 4),
            *[trade(rhs[block * rows : (block + 1) * rows], k) for k in range(1, members)],
            partial,
            inverse,
            child_update[0],
            columns,
            child_low,
            own_rhs,
        )

    def parent_sends(block):
        part, terms = child_part(block)
        (child_root,) = call(
            functools.partial(child_root_kernel, parent_size // LOW),
            [((rows, root_size), BF)],
            [pltpu.VMEM((8 * rows, child_width), BF)],
            8 << 20,
            (rows * 2 * root_size * child_width, root_size * rows * 4),
            terms,
            columns,
            child_low,
        )
        steps = [1 << bit for bit in range((group - 1).bit_length())]
        for step in steps if block else reversed(steps):
            part = (part.astype(F32) + trade(part, step).astype(F32)).astype(BF)
        return call(
            functools.partial(parent_kernel, group, where),
            [((rows, 2 * root_share), BF)] * group,
            [
                pltpu.VMEM((rows, parent_width), BF),
                pltpu.VMEM((8 * rows, parent_width), BF),
                pltpu.VMEM((rows, root_size), BF),
            ],
            8 << 20,
            (rows * 2 * root_size * parent_width, parent_update.size * 4),
            -part,
            parent_inverse[0],
            parent_update[0],
            parent_columns,
            parent_low,
            child_root,
        )

    def group_sum(parts, block, after=()):
        arrived = [trade(parts[k], k) for k in range(1, group)]
        own = parts[0]
        if after:
            *_, own = lax.optimization_barrier((*after, own))
        total = own.astype(F32) - placed_rhs[block * rows : (block + 1) * rows]
        if after:
            total, arrived = lax.optimization_barrier((total, arrived))
        for value in arrived:
            total = total + value.astype(F32)
        return total

    early_ones = (0, *range(2, group))
    late_ones = (1,)

    def gathered(now):
        pieces = [now] + [trade(now, k) for k in range(1, group)]
        (early,) = call(
            functools.partial(early_root_kernel, group, where, early_ones),
            [((rows, root_share), F32)],
            [],
            4 << 20,
            root_cost,
            *[pieces[k] for k in early_ones],
            root_inverse[0],
        )
        return [pieces[k] for k in late_ones] + [root_inverse[0], early]

    def crossed(part, narrow):
        return part + trade(narrow, group).astype(F32)

    root_cost = (rows * root_inverse.size, root_inverse.size)
    part = group_sum(parent_sends(0), 0)
    now = (-crossed(part, part.astype(BF)) * keep).astype(BF)
    part = group_sum(parent_sends(1), 1, (now,))
    total = crossed(part, part.astype(BF))
    first_sol, outgoing = call(
        functools.partial(first_root_kernel, group, where, late_ones),
        [((rows, root_share), BF), ((rows, root_share), BF)],
        [],
        4 << 20,
        root_cost,
        *gathered(now),
        coupling,
    )
    places = [(one, d) for one in range(layers) for d in range(devices)]
    same = [(g * devices + d, (g + 1) % layers * devices + d) for g, d in places]
    over = [
        (g * devices + d, ((g + 1) % layers if d < group else g) * devices + (d ^ group))
        for g, d in places
    ]
    incoming = lax.ppermute(outgoing, ("layer", "front"), same).astype(F32)
    beside = lax.ppermute(outgoing, ("layer", "front"), over).astype(F32)
    arrived = jnp.concatenate([incoming * lower_in + beside * upper_in, incoming * upper_in], 1)
    now = -(total + arrived) * keep
    (out,) = call(
        functools.partial(second_root_kernel, group, where, late_ones),
        [((both, root_share), BF)],
        [],
        4 << 20,
        root_cost,
        *gathered(now.astype(BF)),
        first_sol,
    )
    return out.reshape(1, 2, rows, root_share)


def solution(mesh):
    placed = (
        P("layer", None, None, "front"),
        P("layer", None, None, "front"),
        P("layer", None, None, "front"),
        P("layer", None, "front"),
        P("layer", "front", None),
        P("layer", None, "front"),
        P("layer", "front", None),
        P("layer", None, "front"),
        P("layer", "front"),
        P(),
        P(),
    )

    return jax.shard_map(
        body, mesh=mesh, in_specs=placed, out_specs=P("layer", None, None, "front"), check_vma=False
    )
```
